32 devices in a mesh: blk: 4 (over y, x), grp: 8 (over z, core).
Axes of the slice: x: 2, y: 2, z: 4, core: 2. Of those that a mesh axis runs over, the one named last changes fastest.
Arguments:
- h_blocks: bfloat16 [1536, 16, 128, 128], P(('blk', 'grp')), may hold values from -0.0625 to 0.0625
- h_cols: int32 [1536, 16], P(('blk', 'grp')), may hold values from 0 to 1535, as said below
- t_prev: bfloat16 [196608, 128], P(('blk', 'grp')), may hold values from -6 to 6
- t_cur: bfloat16 [196608, 128], P(('blk', 'grp')), may hold values from -6 to 6
- cheb_coeffs: float32 [3], replicated, may hold values from 0.4 to 1
- owner_slot: int32 [128], replicated, may hold values from 0 to 127, each once
Outputs:
- t_next: bfloat16 [196608, 128], P(('blk', 'grp'))
- t_last: bfloat16 [196608, 128], P(('blk', 'grp'))
- owner_density: float32 [128, 196608], P(('blk', 'grp'))
The draws below stay inside these ranges and needn't reach their ends.
Inputs may be any that keep to these rules, and one draw needn't show every extreme that they name: Block column h_cols[i, k] lies within 24 block rows of i, counted around the ends (periodically); distances of exactly 24 occur both ways; a name may repeat within a row. `owner_slot`: each row of the owner layout receives exactly one window column.
All inputs are finite; a program needn't handle non-finite values.
Results may differ from the reference program's by a relative error of at most 0.009.
Values may be sent and summed in bfloat16 or wider, within the bound.
A program may use at most 192 MiB of HBM per device.

```python
import jax
import jax.numpy as jnp
from jax import lax

BS = 128
NBLK = 1536
KNZ = 16
COLS = 128
ORDER = 196608
REACH = 24


def draw_h_cols(key, part):
    offsets = jax.random.randint(key, (NBLK, KNZ), -REACH, REACH + 1)
    offsets = offsets.at[0, 0].set(-1).at[0, 1].set(REACH).at[0, 2].set(-REACH).at[1, 0].set(-1)
    rows = jnp.arange(NBLK, dtype=jnp.int32)[:, None]
    return ((rows + offsets) % NBLK).astype(jnp.int32)


def shard_levels(key, extent, cuts, low, high):
    gain, own = 1.0, jax.random.fold_in(key, 6)
    for position, shards_of in cuts:
        heights = jnp.exp(jax.random.uniform(jax.random.fold_in(own, position), (shards_of,), jnp.float32, low / len(cuts), high / len(cuts)))
        gain = gain * jnp.repeat(heights, extent[position] // shards_of).reshape([-1 if axis == position else 1 for axis in range(len(extent))])
    return gain


def bell_draw(own_key, shape, scale, reach, pieces=(), kind=jnp.bfloat16):
    loudness = shard_levels(own_key, shape, pieces, -0.22, 0.18) if pieces else 1.0
    result = jax.random.normal(own_key, shape, jnp.float32) * scale * loudness
    return jnp.minimum(jnp.maximum(result, -reach), reach).astype(kind)


def setup_inputs(seed: int = 0) -> dict:
    streams_of = jax.random.split(jax.random.key(seed), 7)
    return {
        "h_blocks": bell_draw(streams_of[0], (NBLK, KNZ, BS, BS), (4 * KNZ * BS) ** -0.5, 0.0625, ((0, 32),)),
        "h_cols": draw_h_cols(jax.random.fold_in(streams_of[6], 71), 0),
        "t_prev": bell_draw(streams_of[2], (ORDER, COLS), 1.0, 6.0, ((0, 32),)),
        "t_cur": bell_draw(streams_of[3], (ORDER, COLS), 1.0, 6.0, ((0, 32),)),
        "cheb_coeffs": jnp.clip(jax.random.uniform(streams_of[4], (3,), jnp.float32, 0.4, 1.0), 0.4, 1.0),
        "owner_slot": jax.random.permutation(streams_of[5], COLS).astype(jnp.int32),
    }


def apply_h(h_blocks, h_cols, current):
    blocks = current.reshape(NBLK, BS, COLS)

    def one_slot(total, slot):
        picked = jnp.take(blocks, jnp.take(h_cols, slot, axis=1), axis=0).astype(jnp.float32)
        tile = jnp.take(h_blocks, slot, axis=1).astype(jnp.float32)
        return total + jnp.einsum('iab,ibm->iam', tile, picked), None

    total, unused = lax.scan(one_slot, jnp.zeros((NBLK, BS, COLS), jnp.float32), jnp.arange(KNZ, dtype=jnp.int32))
    return total.reshape(NBLK * BS, COLS)


def reference(h_blocks, h_cols, t_prev, t_cur, cheb_coeffs, owner_slot):
    before, current = t_prev, t_cur
    made = []
    for term in range(3):
        fresh = (2.0 * apply_h(h_blocks, h_cols, current) - before.astype(jnp.float32)).astype(jnp.bfloat16)
        made.append(fresh)
        before, current = current, fresh
    density = cheb_coeffs[0] * made[0].astype(jnp.float32)
    density = density + cheb_coeffs[1] * made[1].astype(jnp.float32)
    density = density + cheb_coeffs[2] * made[2].astype(jnp.float32)
    owner_density = jnp.zeros((COLS, NBLK * BS), jnp.float32).at[owner_slot].set(density.T)
    return made[1], made[2], owner_density
```

```python
import functools

import jax
import jax.numpy as jnp
from jax import lax
from jax.experimental import pallas as pl
from jax.experimental.pallas import tpu as pltpu
from jax.sharding import PartitionSpec as P

AXES = ("blk", "grp")


def row_product(cols, row, slots, h_row, ext):
    rhs = jnp.concatenate([ext[cols[row * slots + k]] for k in range(slots)], axis=0)
    lhs = jnp.concatenate([h_row(k) for k in range(slots)], axis=1)
    return jnp.dot(lhs, rhs, preferred_element_type=jnp.float32)


def term_kernel(group, slots, cols, h_ref, prev_ref, before, cur, after, out_ref, ext, sems):
    step = pl.program_id(0)
    reach, rows = before.shape[0], cur.shape[0]

    @pl.when(step == 0)
    def _():
        copies = [
            pltpu.make_async_copy(before, ext.at[pl.ds(0, reach)], sems.at[0]),
            pltpu.make_async_copy(cur, ext.at[pl.ds(reach, rows)], sems.at[1]),
            pltpu.make_async_copy(after, ext.at[pl.ds(reach + rows, reach)], sems.at[2]),
        ]
        for c in copies:
            c.start()
        for c in copies:
            c.wait()

    for r in range(group):
        total = row_product(cols, step * group + r, slots, lambda k: h_ref[r, k], ext)
        out_ref[r] = (2.0 * total - prev_ref[r].astype(jnp.float32)).astype(out_ref.dtype)


def apply_term(cols, h_blocks, prev, before, cur, after):
    rows, slots, bs, _ = h_blocks.shape
    width = cur.shape[2]
    reach = before.shape[0]
    group = 4 if rows % 4 == 0 else 1
    anyspec = pl.BlockSpec(memory_space=pl.ANY)
    return pl.pallas_call(
        functools.partial(term_kernel, group, slots),
        out_shape=jax.ShapeDtypeStruct(cur.shape, cur.dtype),
        grid_spec=pltpu.PrefetchScalarGridSpec(
            num_scalar_prefetch=1,
            grid=(rows // group,),
            in_specs=[
                pl.BlockSpec((group, slots, bs, bs), lambda i, c: (i, 0, 0, 0)),
                pl.BlockSpec((group, bs, width), lambda i, c: (i, 0, 0)),
                anyspec,
                anyspec,
                anyspec,
            ],
            out_specs=pl.BlockSpec((group, bs, width), lambda i, c: (i, 0, 0)),
            scratch_shapes=[
                pltpu.VMEM((rows + 2 * reach, bs, width), cur.dtype),
                pltpu.SemaphoreType.DMA((3,)),
            ],
        ),
        name="term",
    )(cols, h_blocks, prev, before, cur, after)


def fill_chooser(chooser, owner, per_dev, group):
    shape = chooser.shape
    width = shape[1] // group
    q = lax.broadcasted_iota(jnp.int32, shape, 0)
    j = lax.broadcasted_iota(jnp.int32, shape, 1)
    span = group * per_dev
    slot = (q // span) * per_dev + q % per_dev
    hit = ((q % span) // per_dev == j // width) & (slot == owner)
    chooser[...] = jnp.where(hit, 1.0, 0.0).astype(chooser.dtype)


def pack_kernel(group, per_dev, coeffs, owner, a_ref, b_ref, c_ref, out_ref, chooser):
    @pl.when(pl.program_id(0) == 0)
    def _():
        fill_chooser(chooser, owner[...], per_dev, group)

    parts = []
    for b in range(group):
        dens = coeffs[0] * a_ref[b].astype(jnp.float32)
        dens = dens + coeffs[1] * b_ref[b].astype(jnp.float32)
        dens = dens + coeffs[2] * c_ref[b].astype(jnp.float32)
        parts.append(dens.astype(jnp.bfloat16))
    dens = jnp.concatenate(parts, axis=1)
    packed = lax.dot_general(chooser[...], dens, (((1,), (1,)), ((), ())), preferred_element_type=jnp.float32)
    out_ref[...] = packed.reshape(out_ref.shape).astype(out_ref.dtype)


def pack_group(rows, per_dev):
    group = max(1, 16 // per_dev)
    return group if rows % group == 0 else rows


def pack_density(coeffs, owner_slot, made, devices):
    rows, bs, width = made[0].shape
    per_dev = width // devices
    group = pack_group(rows, per_dev)
    tspec = pl.BlockSpec((group, bs, width), lambda i, c: (i, 0, 0))
    return pl.pallas_call(
        functools.partial(pack_kernel, group, per_dev),
        out_shape=jax.ShapeDtypeStruct((devices, rows * per_dev, bs), jnp.bfloat16),
        grid_spec=pltpu.PrefetchScalarGridSpec(
            num_scalar_prefetch=1,
            grid=(rows // group,),
            in_specs=[pl.BlockSpec((1, group * width), lambda i, c: (0, 0)), tspec, tspec, tspec],
            out_specs=pl.BlockSpec((devices, group * per_dev, bs), lambda i, c: (0, i, 0)),
            scratch_shapes=[pltpu.VMEM((devices * group * per_dev, group * width), jnp.bfloat16)],
        ),
        name="pack",
    )(coeffs, jnp.tile(owner_slot, group)[None, :], *made)


def on_device(h_blocks, h_cols, t_prev, t_cur, cheb_coeffs, owner_slot):
    rows, slots, bs, _ = h_blocks.shape
    width = t_cur.shape[1]
    devices = lax.axis_size(AXES)
    reach = rows // 2
    first_row = lax.axis_index(AXES) * rows
    local_cols = ((h_cols - first_row + reach) % (rows * devices)).reshape(-1)
    up = [(i, (i + 1) % devices) for i in range(devices)]
    down = [(j, i) for i, j in up]
    before, current = (t_prev.reshape(rows, bs, width), t_cur.reshape(rows, bs, width))
    made = []
    for _ in range(3):
        left = lax.ppermute(current[rows - reach :], AXES, up)
        right = lax.ppermute(current[:reach], AXES, down)
        fresh = apply_term(local_cols, h_blocks, before, left, current, right)
        made.append(fresh)
        before, current = (current, fresh)
    packed = pack_density(cheb_coeffs, owner_slot, made, devices)
    arrived = lax.all_to_all(packed, AXES, split_axis=0, concat_axis=0, tiled=True)
    per_dev = width // devices
    owned = arrived.astype(jnp.float32).reshape(devices * rows, per_dev, bs)
    owned = owned.transpose(1, 0, 2).reshape(per_dev, devices * rows * bs)
    return (made[1].reshape(-1, width), made[2].reshape(-1, width), owned)


def solution(mesh):
    return jax.shard_map(
        on_device,
        mesh=mesh,
        in_specs=(
            P(("blk", "grp"), None, None, None),
            P(("blk", "grp"), None),
            P(("blk", "grp"), None),
            P(("blk", "grp"), None),
            P(),
            P(),
        ),
        out_specs=(P(("blk", "grp"), None), P(("blk", "grp"), None), P(("blk", "grp"), None)),
        check_vma=False,
    )
```

```python
import functools

import jax
import jax.numpy as jnp
from jax import lax
from jax.experimental import pallas as pl
from jax.experimental.pallas import tpu as pltpu
from jax.sharding import PartitionSpec as P

AXES = ("blk", "grp")

MESH = pl.DeviceIdType.MESH


def row_product(cols, row, h_ref, ext):
    slots = h_ref.shape[1]
    rhs = jnp.concatenate([ext[cols[row * slots + k]] for k in range(slots)], axis=0)
    lhs = jnp.concatenate([h_ref[row, k] for k in range(slots)], axis=1)
    return jnp.dot(lhs, rhs, preferred_element_type=jnp.float32)


def whole_kernel(
    shape, cols, coeffs, owner, h_hbm, prev_hbm, cur_hbm, next_out, last_out, arrived,
    h_ref, ext_a, ext_b, ext_c, prev_ref, last_ref, packed, stage, chooser,
    load_sem, h_sem, send_sem, recv_sem, spread_sem, gather_sem, out_sem,
):
    reach, pieces, per_dev, group = shape
    rows, _, bs, width = h_ref.shape[0], h_ref.shape[1], h_ref.shape[2], ext_a.shape[2]
    piece = reach // pieces
    blks, grps = lax.axis_size("blk"), lax.axis_size("grp")
    devices = blks * grps
    blk, grp = lax.axis_index("blk"), lax.axis_index("grp")
    me = blk * grps + grp

    def place(linear):
        return (linear // grps, linear % grps)

    def base_of(c):
        return (c % 2) * reach + (c // 2) * piece

    def h_load(c):
        where = pl.ds(base_of(c), piece)
        return pltpu.make_async_copy(h_hbm.at[where], h_ref.at[where], h_sem.at[c])

    def halo(term, source, offset, dest, c):
        side = c % 2
        there = (1 - side) * (reach + rows) + (c // 2) * piece
        return pltpu.make_async_remote_copy(
            src_ref=source.at[pl.ds(offset + base_of(c), piece)],
            dst_ref=dest.at[pl.ds(there, piece)],
            send_sem=send_sem.at[term, c],
            recv_sem=recv_sem.at[term, c],
            device_id=place((me + devices - 1 + 2 * side) % devices),
            device_id_type=MESH,
        )

    prev_load = pltpu.make_async_copy(prev_hbm, prev_ref, load_sem.at[0])
    cur_load = pltpu.make_async_copy(cur_hbm, ext_a.at[pl.ds(reach, rows)], load_sem.at[1])
    cur_load.start()
    prev_load.start()

    barrier = pltpu.get_barrier_semaphore()

    def greet(i, carry):
        pl.semaphore_signal(barrier, inc=1, device_id=place((me + i) % devices), device_id_type=MESH)
        return carry

    lax.fori_loop(1, devices, greet, 0)
    for c in range(2 * pieces):
        h_load(c).start()

    q = lax.broadcasted_iota(jnp.int32, chooser.shape, 0)
    slot = (q % devices) * per_dev + q // devices
    chooser[...] = jnp.where(slot == owner[...], 1.0, 0.0).astype(chooser.dtype)

    pl.semaphore_wait(barrier, devices - 1)
    for c in range(2 * pieces):
        halo(0, cur_hbm, 0, ext_a, c).start()
    prev_load.wait()
    cur_load.wait()

    def run_term(term, ext, old, old_at, new, new_at, ready, done):
        for c in range(2 * pieces):
            if term == 0:
                halo(0, cur_hbm, 0, ext_a, c).wait()
            else:
                halo(term, ext, reach, ext, c).wait()

        def one_piece(c, carry):
            base = base_of(c)
            ready(c)

            def one_row(r, inner):
                row = base + r
                total = row_product(cols, row, h_ref, ext)
                fresh = 2.0 * total - old[old_at + row].astype(jnp.float32)
                new[new_at + row] = fresh.astype(new.dtype)
                return inner

            lax.fori_loop(0, piece, one_row, 0)
            done(c)
            return carry

        lax.fori_loop(0, 2 * pieces, one_piece, 0)

    def nothing(c):
        pass

    run_term(
        0, ext_a, prev_ref, 0, ext_b, reach,
        lambda c: h_load(c).wait(), lambda c: halo(1, ext_b, reach, ext_b, c).start(),
    )
    run_term(
        1, ext_b, ext_a, reach, ext_c, reach,
        nothing, lambda c: halo(2, ext_c, reach, ext_c, c).start(),
    )
    next_store = pltpu.make_async_copy(ext_c.at[pl.ds(reach, rows)], next_out, out_sem.at[0])
    next_store.start()

    def pack(first):
        for b in range(group):
            row = first + b
            dens = coeffs[0] * ext_b[reach + row].astype(jnp.float32)
            dens = dens + coeffs[1] * ext_c[reach + row].astype(jnp.float32)
            dens = dens + coeffs[2] * last_ref[row].astype(jnp.float32)
            turned = lax.dot_general(
                chooser[...], dens.astype(jnp.bfloat16), (((1,), (1,)), ((), ())),
                preferred_element_type=jnp.float32,
            )
            for s in range(per_dev):
                stage[pl.ds(b * per_dev + s, devices, stride=group * per_dev), :] = turned[
                    s * devices : (s + 1) * devices
                ]
        span = group * per_dev
        tiles = stage[...].reshape(devices, span, bs).astype(packed.dtype)
        packed[:, pl.ds(pl.multiple_of(first * per_dev, span), span), :] = tiles

    def spread(base, count):
        where = pl.ds(base * per_dev, count * per_dev)

        def one(i, carry):
            k = i // blks
            turn = (grps // 2 + (1 - 2 * (k % 2)) * ((k + 1) // 2) + grps) % grps
            to_blk = (blk + i + 1) % blks
            to_grp = (grp + turn) % grps
            pltpu.make_async_remote_copy(
                src_ref=packed.at[to_blk * grps + to_grp, where],
                dst_ref=arrived.at[me, where],
                send_sem=spread_sem,
                recv_sem=gather_sem,
                device_id=(to_blk, to_grp),
                device_id_type=MESH,
            ).start()
            return carry

        lax.fori_loop(0, devices - 1, one, 0)

    interleaved = piece % group == 0

    def last_done(c):
        if interleaved:
            base = base_of(c)

            def one_group(g, carry):
                pack(base + g * group)
                return carry

            lax.fori_loop(0, piece // group, one_group, 0)
            spread(base, piece)

    run_term(2, ext_c, ext_b, reach, last_ref, 0, nothing, last_done)
    last_store = pltpu.make_async_copy(last_ref, last_out, out_sem.at[1])
    last_store.start()
    if not interleaved:
        for g in range(rows // group):
            pack(g * group)
        spread(0, rows)
    own = pltpu.make_async_copy(packed.at[me], arrived.at[me], out_sem.at[2])
    own.start()
    everything = pltpu.make_async_remote_copy(
        src_ref=packed.at[pl.ds(0, devices - 1)],
        dst_ref=arrived.at[pl.ds(0, devices - 1)],
        send_sem=spread_sem,
        recv_sem=gather_sem,
        device_id=place((me + 1) % devices),
        device_id_type=MESH,
    )
    everything.wait()
    own.wait()
    next_store.wait()
    last_store.wait()


def on_device(h_blocks, h_cols, t_prev, t_cur, cheb_coeffs, owner_slot):
    rows, slots, bs, _ = h_blocks.shape
    width = t_cur.shape[1]
    devices = lax.axis_size(AXES)
    reach = rows // 2
    per_dev = width // devices
    pieces = 3 if reach % 3 == 0 else 1
    group = max(1, 16 // per_dev)
    group = group if rows % group == 0 else rows
    first_row = lax.axis_index(AXES) * rows
    local_cols = ((h_cols - first_row + reach) % (rows * devices)).reshape(-1)
    anyspec = pl.BlockSpec(memory_space=pl.ANY)
    smem = pl.BlockSpec(memory_space=pltpu.SMEM)
    vmem = pl.BlockSpec(memory_space=pltpu.VMEM)
    dma = pltpu.SemaphoreType.DMA
    term = jax.ShapeDtypeStruct((rows, bs, width), t_cur.dtype)
    ext = pltpu.VMEM((rows + 2 * reach, bs, width), t_cur.dtype)
    own = pltpu.VMEM((rows, bs, width), t_cur.dtype)
    made_next, made_last, arrived = pl.pallas_call(
        functools.partial(whole_kernel, (reach, pieces, per_dev, group)),
        out_shape=(term, term, jax.ShapeDtypeStruct((devices, rows * per_dev, bs), jnp.bfloat16)),
        in_specs=[smem, smem, vmem, anyspec, anyspec, anyspec],
        out_specs=(anyspec, anyspec, anyspec),
        scratch_shapes=[
            pltpu.VMEM(h_blocks.shape, h_blocks.dtype),
            ext,
            ext,
            ext,
            own,
            own,
            pltpu.VMEM((devices, rows * per_dev, bs), jnp.bfloat16),
            pltpu.VMEM((devices * group * per_dev, bs), jnp.float32),
            pltpu.VMEM((width, width), jnp.bfloat16),
            dma((2,)),
            dma((2 * pieces,)),
            dma((3, 2 * pieces)),
            dma((3, 2 * pieces)),
            dma,
            dma,
            dma((3,)),
        ],
        compiler_params=pltpu.CompilerParams(collective_id=0, has_side_effects=True, vmem_limit_bytes=58 * 1024 * 1024),
        name="whole",
    )(
        local_cols,
        cheb_coeffs,
        owner_slot[None, :],
        h_blocks,
        t_prev.reshape(rows, bs, width),
        t_cur.reshape(rows, bs, width),
    )
    owned = arrived.astype(jnp.float32).reshape(devices * rows, per_dev, bs)
    owned = owned.transpose(1, 0, 2).reshape(per_dev, devices * rows * bs)
    return (made_next.reshape(-1, width), made_last.reshape(-1, width), owned)


def solution(mesh):
    return jax.shard_map(
        on_device,
        mesh=mesh,
        in_specs=(
            P(("blk", "grp"), None, None, None),
            P(("blk", "grp"), None),
            P(("blk", "grp"), None),
            P(("blk", "grp"), None),
            P(),
            P(),
        ),
        out_specs=(P(("blk", "grp"), None), P(("blk", "grp"), None), P(("blk", "grp"), None)),
        check_vma=False,
    )
```

```python
import functools

import jax
import jax.numpy as jnp
from jax import lax
from jax.experimental import pallas as pl
from jax.experimental.pallas import tpu as pltpu
from jax.sharding import PartitionSpec as P

AXES = ("blk", "grp")

MESH = pl.DeviceIdType.MESH


def row_product(cols, row, h_ref, ext):
    slots = h_ref.shape[1]
    rhs = jnp.concatenate([ext[cols[row, k]] for k in range(slots)], axis=0)
    lhs = jnp.concatenate([h_ref[row, k] for k in range(slots)], axis=1)
    return jnp.dot(lhs, rhs, preferred_element_type=jnp.float32)


def whole_kernel(
    shape, h_cols, coeffs, owner, h_hbm, prev_hbm, cur_hbm, next_out, last_out, arrived,
    h_ref, ext_a, ext_b, ext_c, prev_ref, last_ref, packed, stage, chooser, cols,
    load_sem, h_sem, send_sem, recv_sem, spread_sem, gather_sem, out_sem,
):
    reach, pieces, per_dev, group = shape
    rows, _, bs, width = h_ref.shape[0], h_ref.shape[1], h_ref.shape[2], ext_a.shape[2]
    piece = reach // pieces
    blks, grps = lax.axis_size("blk"), lax.axis_size("grp")
    devices = blks * grps
    blk, grp = lax.axis_index("blk"), lax.axis_index("grp")
    me = blk * grps + grp

    def place(linear):
        return (linear // grps, linear % grps)

    first_side = grp % 2

    def side_of(c):
        return (first_side + c // pieces) % 2

    def base_of(c):
        return side_of(c) * reach + (c % pieces) * piece

    def h_load(c):
        where = pl.ds(base_of(c), piece)
        return pltpu.make_async_copy(h_hbm.at[where], h_ref.at[where], h_sem.at[c])

    def halo(term, source, offset, dest, c):
        side = side_of(c)
        there = (1 - side) * (reach + rows) + (c % pieces) * piece
        return pltpu.make_async_remote_copy(
            src_ref=source.at[pl.ds(offset + base_of(c), piece)],
            dst_ref=dest.at[pl.ds(there, piece)],
            send_sem=send_sem.at[term, side, c % pieces],
            recv_sem=recv_sem.at[term, side, c % pieces],
            device_id=place((me + devices - 1 + 2 * side) % devices),
            device_id_type=MESH,
        )

    prev_load = pltpu.make_async_copy(prev_hbm, prev_ref, load_sem.at[0])
    cur_load = pltpu.make_async_copy(cur_hbm, ext_a.at[pl.ds(reach, rows)], load_sem.at[1])
    cur_load.start()
    prev_load.start()

    barrier = pltpu.get_barrier_semaphore()

    def greet(i, carry):
        pl.semaphore_signal(barrier, inc=1, device_id=place((me + i) % devices), device_id_type=MESH)
        return carry

    lax.fori_loop(1, devices, greet, 0)
    for c in range(2 * pieces):
        h_load(c).start()

    q = lax.broadcasted_iota(jnp.int32, chooser.shape, 0)
    slot = (q % devices) * per_dev + q // devices
    chooser[...] = jnp.where(slot == owner[...], 1.0, 0.0).astype(chooser.dtype)

    pl.semaphore_wait(barrier, devices - 1)
    for c in range(2 * pieces):
        halo(0, cur_hbm, 0, ext_a, c).start()
    total_rows = rows * devices

    def local_row(row, carry):
        for k in range(h_ref.shape[1]):
            at = h_cols[row, k] - me * rows + reach
            at = jnp.where(at < 0, at + total_rows, at)
            at = jnp.where(at >= total_rows, at - total_rows, at)
            cols[row, k] = jnp.clip(at, 0, rows + 2 * reach - 1)
        return carry

    lax.fori_loop(0, rows, local_row, 0)
    prev_load.wait()
    cur_load.wait()

    def run_term(term, ext, old, old_at, new, new_at, ready, done):
        for c in range(2 * pieces):
            if term == 0:
                halo(0, cur_hbm, 0, ext_a, c).wait()
            else:
                halo(term, ext, reach, ext, c).wait()

        def one_piece(c, carry):
            base = base_of(c)
            ready(c)

            for r in range(piece):
                row = base + r
                total = row_product(cols, row, h_ref, ext)
                fresh = 2.0 * total - old[old_at + row].astype(jnp.float32)
                new[new_at + row] = fresh.astype(new.dtype)
            done(c)
            return carry

        lax.fori_loop(0, 2 * pieces, one_piece, 0)

    def nothing(c):
        pass

    run_term(
        0, ext_a, prev_ref, 0, ext_b, reach,
        lambda c: h_load(c).wait(), lambda c: halo(1, ext_b, reach, ext_b, c).start(),
    )
    run_term(
        1, ext_b, ext_a, reach, ext_c, reach,
        nothing, lambda c: halo(2, ext_c, reach, ext_c, c).start(),
    )
    next_store = pltpu.make_async_copy(ext_c.at[pl.ds(reach, rows)], next_out, out_sem.at[0])
    next_store.start()

    def pack(first):
        for b in range(group):
            row = first + b
            dens = coeffs[0] * ext_b[reach + row].astype(jnp.float32)
            dens = dens + coeffs[1] * ext_c[reach + row].astype(jnp.float32)
            dens = dens + coeffs[2] * last_ref[row].astype(jnp.float32)
            turned = lax.dot_general(
                chooser[...], dens.astype(jnp.bfloat16), (((1,), (1,)), ((), ())),
                preferred_element_type=jnp.float32,
            )
            for s in range(per_dev):
                stage[pl.ds(b * per_dev + s, devices, stride=group * per_dev), :] = turned[
                    s * devices : (s + 1) * devices
                ]
        span = group * per_dev
        tiles = stage[...].reshape(devices, span, bs).astype(packed.dtype)
        packed[:, pl.ds(pl.multiple_of(first * per_dev, span), span), :] = tiles

    def spread(base, count):
        where = pl.ds(base * per_dev, count * per_dev)

        def one(i, carry):
            k = i // blks
            turn = (grps // 2 + (1 - 2 * (k % 2)) * ((k + 1) // 2) + grps) % grps
            to_blk = (blk + i + 1) % blks
            to_grp = (grp + turn) % grps
            pltpu.make_async_remote_copy(
                src_ref=packed.at[to_blk * grps + to_grp, where],
                dst_ref=arrived.at[me, where],
                send_sem=spread_sem,
                recv_sem=gather_sem,
                device_id=(to_blk, to_grp),
                device_id_type=MESH,
            ).start()
            return carry

        lax.fori_loop(0, devices - 1, one, 0)

    interleaved = piece % group == 0 and pieces % 2 == 0

    def last_done(c):
        if interleaved:
            base = base_of(c)

            def one_group(g, carry):
                pack(base + g * group)
                return carry

            lax.fori_loop(0, piece // group, one_group, 0)

            @pl.when(c % 2 == 1)
            def _():
                spread(base - piece, 2 * piece)

    run_term(2, ext_c, ext_b, reach, last_ref, 0, nothing, last_done)
    last_store = pltpu.make_async_copy(last_ref, last_out, out_sem.at[1])
    last_store.start()
    if not interleaved:
        for g in range(rows // group):
            pack(g * group)
        spread(0, rows)
    own = pltpu.make_async_copy(packed.at[me], arrived.at[me], out_sem.at[2])
    own.start()
    everything = pltpu.make_async_remote_copy(
        src_ref=packed.at[pl.ds(0, devices - 1)],
        dst_ref=arrived.at[pl.ds(0, devices - 1)],
        send_sem=spread_sem,
        recv_sem=gather_sem,
        device_id=place((me + 1) % devices),
        device_id_type=MESH,
    )
    everything.wait()
    own.wait()
    next_store.wait()
    last_store.wait()


def on_device(h_blocks, h_cols, t_prev, t_cur, cheb_coeffs, owner_slot):
    rows, slots, bs, _ = h_blocks.shape
    width = t_cur.shape[1]
    devices = lax.axis_size(AXES)
    reach = rows // 2
    per_dev = width // devices
    pieces = next(p for p in (6, 3, 2, 1) if reach % p == 0)
    group = max(1, 16 // per_dev)
    group = group if rows % group == 0 else rows
    anyspec = pl.BlockSpec(memory_space=pl.ANY)
    hbm = pl.BlockSpec(memory_space=pltpu.HBM)
    smem = pl.BlockSpec(memory_space=pltpu.SMEM)
    vmem = pl.BlockSpec(memory_space=pltpu.VMEM)
    dma = pltpu.SemaphoreType.DMA
    term = jax.ShapeDtypeStruct((rows, bs, width), t_cur.dtype)
    ext = pltpu.VMEM((rows + 2 * reach, bs, width), t_cur.dtype)
    own = pltpu.VMEM((rows, bs, width), t_cur.dtype)
    made_next, made_last, arrived = pl.pallas_call(
        functools.partial(whole_kernel, (reach, pieces, per_dev, group)),
        out_shape=(term, term, jax.ShapeDtypeStruct((devices, rows * per_dev, bs), jnp.bfloat16)),
        in_specs=[smem, smem, vmem, hbm, hbm, hbm],
        out_specs=(anyspec, anyspec, anyspec),
        scratch_shapes=[
            pltpu.VMEM(h_blocks.shape, h_blocks.dtype),
            ext,
            ext,
            ext,
            own,
            own,
            pltpu.VMEM((devices, rows * per_dev, bs), jnp.bfloat16),
            pltpu.VMEM((devices * group * per_dev, bs), jnp.float32),
            pltpu.VMEM((width, width), jnp.bfloat16),
            pltpu.SMEM((rows, slots), jnp.int32),
            dma((2,)),
            dma((2 * pieces,)),
            dma((3, 2, pieces)),
            dma((3, 2, pieces)),
            dma,
            dma,
            dma((3,)),
        ],
        compiler_params=pltpu.CompilerParams(collective_id=0, has_side_effects=True, vmem_limit_bytes=42 * 1024 * 1024),
        name="whole",
    )(
        h_cols,
        cheb_coeffs,
        owner_slot[None, :],
        h_blocks,
        pltpu.with_memory_space_constraint(t_prev.reshape(rows, bs, width), pltpu.HBM),
        pltpu.with_memory_space_constraint(t_cur.reshape(rows, bs, width), pltpu.HBM),
    )
    owned = arrived.astype(jnp.float32).reshape(devices * rows, per_dev, bs)
    owned = owned.transpose(1, 0, 2).reshape(per_dev, devices * rows * bs)
    return (made_next.reshape(-1, width), made_last.reshape(-1, width), owned)


def solution(mesh):
    return jax.shard_map(
        on_device,
        mesh=mesh,
        in_specs=(
            P(("blk", "grp"), None, None, None),
            P(("blk", "grp"), None),
            P(("blk", "grp"), None),
            P(("blk", "grp"), None),
            P(),
            P(),
        ),
        out_specs=(P(("blk", "grp"), None), P(("blk", "grp"), None), P(("blk", "grp"), None)),
        check_vma=False,
    )
```

```python
import functools

import jax
import jax.numpy as jnp
from jax import lax
from jax.experimental import pallas as pl
from jax.experimental.pallas import tpu as pltpu
from jax.sharding import PartitionSpec as P

AXES = ("blk", "grp")

MESH = pl.DeviceIdType.MESH


def row_product(cols, row, h_ref, ext):
    slots = h_ref.shape[1]
    rhs = jnp.concatenate([ext[cols[row, k]] for k in range(slots)], axis=0)
    lhs = jnp.concatenate([h_ref[row, k] for k in range(slots)], axis=1)
    return jnp.dot(lhs, rhs, preferred_element_type=jnp.float32)


def whole_kernel(
    shape, h_cols, coeffs, owner, h_hbm, prev_hbm, cur_hbm, next_out, last_out, arrived,
    h_ref, ext_a, ext_b, ext_c, prev_ref, last_ref, packed, stage, chooser, cols,
    load_sem, h_sem, send_sem, recv_sem, spread_sem, gather_sem, out_sem,
):
    reach, pieces, per_dev, group = shape
    rows, _, bs, width = h_ref.shape[0], h_ref.shape[1], h_ref.shape[2], ext_a.shape[2]
    piece = reach // pieces
    blks, grps = lax.axis_size("blk"), lax.axis_size("grp")
    devices = blks * grps
    blk, grp = lax.axis_index("blk"), lax.axis_index("grp")
    me = blk * grps + grp

    def place(linear):
        return (linear // grps, linear % grps)

    first_side = grp % 2

    def side_of(c):
        return (first_side + c // pieces) % 2

    def base_of(c):
        return side_of(c) * reach + (c % pieces) * piece

    def h_load(c):
        where = pl.ds(base_of(c), piece)
        return pltpu.make_async_copy(h_hbm.at[where], h_ref.at[where], h_sem.at[c])

    def halo(term, source, offset, dest, c):
        side = side_of(c)
        there = (1 - side) * (reach + rows) + (c % pieces) * piece
        return pltpu.make_async_remote_copy(
            src_ref=source.at[pl.ds(offset + base_of(c), piece)],
            dst_ref=dest.at[pl.ds(there, piece)],
            send_sem=send_sem.at[term, side, c % pieces],
            recv_sem=recv_sem.at[term, side, c % pieces],
            device_id=place((me + devices - 1 + 2 * side) % devices),
            device_id_type=MESH,
        )

    prev_load = pltpu.make_async_copy(prev_hbm, prev_ref, load_sem.at[0])
    cur_load = pltpu.make_async_copy(cur_hbm, ext_a.at[pl.ds(reach, rows)], load_sem.at[1])
    cur_load.start()
    prev_load.start()

    barrier = pltpu.get_barrier_semaphore()

    def greet(i, carry):
        pl.semaphore_signal(barrier, inc=1, device_id=place((me + i) % devices), device_id_type=MESH)
        return carry

    lax.fori_loop(1, devices, greet, 0)
    for c in range(2 * pieces):
        h_load(c).start()

    q = lax.broadcasted_iota(jnp.int32, chooser.shape, 0)
    slot = (q % devices) * per_dev + q // devices
    chooser[...] = jnp.where(slot == owner[...], 1.0, 0.0).astype(chooser.dtype)

    pl.semaphore_wait(barrier, devices - 1)
    for c in range(2 * pieces):
        halo(0, cur_hbm, 0, ext_a, c).start()
    total_rows = rows * devices

    def local_row(row, carry):
        for k in range(h_ref.shape[1]):
            at = h_cols[k, row] - me * rows + reach
            at = jnp.where(at < 0, at + total_rows, at)
            at = jnp.where(at >= total_rows, at - total_rows, at)
            cols[row, k] = jnp.clip(at, 0, rows + 2 * reach - 1)
        return carry

    lax.fori_loop(0, rows, local_row, 0)
    prev_load.wait()
    cur_load.wait()

    def run_term(term, ext, old, old_at, new, new_at, ready, done):
        for c in range(2 * pieces):
            if term == 0:
                halo(0, cur_hbm, 0, ext_a, c).wait()
            else:
                halo(term, ext, reach, ext, c).wait()

        def one_piece(c, carry):
            base = base_of(c)
            ready(c)

            for r in range(piece):
                row = base + r
                total = row_product(cols, row, h_ref, ext)
                fresh = 2.0 * total - old[old_at + row].astype(jnp.float32)
                new[new_at + row] = fresh.astype(new.dtype)
            done(c)
            return carry

        lax.fori_loop(0, 2 * pieces, one_piece, 0)

    def nothing(c):
        pass

    run_term(
        0, ext_a, prev_ref, 0, ext_b, reach,
        lambda c: h_load(c).wait(), lambda c: halo(1, ext_b, reach, ext_b, c).start(),
    )
    run_term(
        1, ext_b, ext_a, reach, ext_c, reach,
        nothing, lambda c: halo(2, ext_c, reach, ext_c, c).start(),
    )
    next_store = pltpu.make_async_copy(ext_c.at[pl.ds(reach, rows)], next_out, out_sem.at[0])
    next_store.start()

    def pack(first):
        for b in range(group):
            row = first + b
            dens = coeffs[0] * ext_b[reach + row].astype(jnp.float32)
            dens = dens + coeffs[1] * ext_c[reach + row].astype(jnp.float32)
            dens = dens + coeffs[2] * last_ref[row].astype(jnp.float32)
            turned = lax.dot_general(
                chooser[...], dens.astype(jnp.bfloat16), (((1,), (1,)), ((), ())),
                preferred_element_type=jnp.float32,
            )
            for s in range(per_dev):
                stage[pl.ds(b * per_dev + s, devices, stride=group * per_dev), :] = turned[
                    s * devices : (s + 1) * devices
                ]
        span = group * per_dev
        tiles = stage[...].reshape(devices, span, bs).astype(packed.dtype)
        packed[:, pl.ds(pl.multiple_of(first * per_dev, span), span), :] = tiles

    def spread(base, count):
        where = pl.ds(base * per_dev, count * per_dev)

        def one(i, carry):
            k = i // blks
            turn = (grps // 2 + (1 - 2 * (k % 2)) * ((k + 1) // 2) + grps) % grps
            to_blk = (blk + i + 1) % blks
            to_grp = (grp + turn) % grps
            pltpu.make_async_remote_copy(
                src_ref=packed.at[to_blk * grps + to_grp, where],
                dst_ref=arrived.at[me, where],
                send_sem=spread_sem,
                recv_sem=gather_sem,
                device_id=(to_blk, to_grp),
                device_id_type=MESH,
            ).start()
            return carry

        lax.fori_loop(0, devices - 1, one, 0)

    interleaved = piece % group == 0 and pieces % 2 == 0

    def last_done(c):
        if interleaved:
            base = base_of(c)

            def one_group(g, carry):
                pack(base + g * group)
                return carry

            lax.fori_loop(0, piece // group, one_group, 0)

            @pl.when(c % 2 == 1)
            def _():
                spread(base - piece, 2 * piece)

    run_term(2, ext_c, ext_b, reach, last_ref, 0, nothing, last_done)
    last_store = pltpu.make_async_copy(last_ref, last_out, out_sem.at[1])
    last_store.start()
    if not interleaved:
        for g in range(rows // group):
            pack(g * group)
        spread(0, rows)
    own = pltpu.make_async_copy(packed.at[me], arrived.at[me], out_sem.at[2])
    own.start()
    everything = pltpu.make_async_remote_copy(
        src_ref=packed.at[pl.ds(0, devices - 1)],
        dst_ref=arrived.at[pl.ds(0, devices - 1)],
        send_sem=spread_sem,
        recv_sem=gather_sem,
        device_id=place((me + 1) % devices),
        device_id_type=MESH,
    )
    everything.wait()
    own.wait()
    next_store.wait()
    last_store.wait()


def in_hbm(array):
    return pltpu.with_memory_space_constraint(array, pltpu.HBM)


def finish_kernel(steps, next_ref, last_ref, arrived, next_out, last_out, owned, sems):
    copies = [
        pltpu.make_async_copy(next_ref, next_out, sems.at[0]),
        pltpu.make_async_copy(last_ref, last_out, sems.at[1]),
    ]

    @pl.when(pl.program_id(0) == 0)
    def _():
        for c in copies:
            c.start()

    owned[...] = arrived[...].astype(owned.dtype)

    @pl.when(pl.program_id(0) == steps - 1)
    def _():
        for c in copies:
            c.wait()


def finish(made_next, made_last, arrived):
    devices, span, bs = arrived.shape
    steps = 4
    anyspec = pl.BlockSpec(memory_space=pl.ANY)
    block = pl.BlockSpec((devices // steps, span, bs), lambda i: (i, 0, 0))
    term = jax.ShapeDtypeStruct(made_next.shape, made_next.dtype)
    return pl.pallas_call(
        functools.partial(finish_kernel, steps),
        out_shape=(term, term, jax.ShapeDtypeStruct(arrived.shape, jnp.float32)),
        grid=(steps,),
        in_specs=[anyspec, anyspec, block],
        out_specs=(anyspec, anyspec, block),
        scratch_shapes=[pltpu.SemaphoreType.DMA((2,))],
        compiler_params=pltpu.CompilerParams(vmem_limit_bytes=16 * 1024 * 1024),
        name="finish",
    )(made_next, made_last, arrived)


def on_device(h_blocks, h_cols, t_prev, t_cur, cheb_coeffs, owner_slot):
    rows, slots, bs, _ = h_blocks.shape
    width = t_cur.shape[1]
    devices = lax.axis_size(AXES)
    reach = rows // 2
    per_dev = width // devices
    pieces = next(p for p in (6, 3, 2, 1) if reach % p == 0)
    group = max(1, 16 // per_dev)
    group = group if rows % group == 0 else rows
    anyspec = pl.BlockSpec(memory_space=pl.ANY)
    hbm = pl.BlockSpec(memory_space=pltpu.HBM)
    smem = pl.BlockSpec(memory_space=pltpu.SMEM)
    vmem = pl.BlockSpec(memory_space=pltpu.VMEM)
    dma = pltpu.SemaphoreType.DMA
    term = jax.ShapeDtypeStruct((rows, bs, width), t_cur.dtype)
    ext = pltpu.VMEM((rows + 2 * reach, bs, width), t_cur.dtype)
    own = pltpu.VMEM((rows, bs, width), t_cur.dtype)
    made_next, made_last, arrived = pl.pallas_call(
        functools.partial(whole_kernel, (reach, pieces, per_dev, group)),
        out_shape=(term, term, jax.ShapeDtypeStruct((devices, rows * per_dev, bs), jnp.bfloat16)),
        in_specs=[smem, smem, vmem, hbm, hbm, hbm],
        out_specs=(anyspec, anyspec, anyspec),
        scratch_shapes=[
            pltpu.VMEM(h_blocks.shape, h_blocks.dtype),
            ext,
            ext,
            ext,
            own,
            own,
            pltpu.VMEM((devices, rows * per_dev, bs), jnp.bfloat16),
            pltpu.VMEM((devices * group * per_dev, bs), jnp.float32),
            pltpu.VMEM((width, width), jnp.bfloat16),
            pltpu.SMEM((rows, slots), jnp.int32),
            dma((2,)),
            dma((2 * pieces,)),
            dma((3, 2, pieces)),
            dma((3, 2, pieces)),
            dma,
            dma,
            dma((3,)),
        ],
        compiler_params=pltpu.CompilerParams(collective_id=0, has_side_effects=True, vmem_limit_bytes=42 * 1024 * 1024),
        name="whole",
    )(
        in_hbm(h_cols.T),
        in_hbm(cheb_coeffs),
        in_hbm(owner_slot[None, :]),
        h_blocks,
        in_hbm(t_prev.reshape(rows, bs, width)),
        in_hbm(t_cur.reshape(rows, bs, width)),
    )
    made_next, made_last, owned = finish(made_next, made_last, arrived)
    owned = owned.reshape(devices * rows, per_dev, bs)
    owned = owned.transpose(1, 0, 2).reshape(per_dev, devices * rows * bs)
    return (made_next.reshape(-1, width), made_last.reshape(-1, width), owned)


def solution(mesh):
    return jax.shard_map(
        on_device,
        mesh=mesh,
        in_specs=(
            P(("blk", "grp"), None, None, None),
            P(("blk", "grp"), None),
            P(("blk", "grp"), None),
            P(("blk", "grp"), None),
            P(),
            P(),
        ),
        out_specs=(P(("blk", "grp"), None), P(("blk", "grp"), None), P(("blk", "grp"), None)),
        check_vma=False,
    )
```
